32 devices in a mesh: ctx: 4 (over z), head: 8 (over y, x, core).
Axes of the slice: x: 2, y: 2, z: 4, core: 2. Of those that a mesh axis runs over, the one named last changes fastest.
Arguments:
- hidden: float32 [1024, 2304], P(('ctx', 'head')), may hold values from -40 to 40
- w_query: float32 [2304, 1536], P(None, 'head'), may hold values from -0.125 to 0.125
- w_down: float32 [2304, 576], replicated, may hold values from -0.125 to 0.125
- latent_gain: float32 [512], replicated, may hold values from 0.25 to 1.75
- w_key_up: float32 [512, 1024], P(None, 'head'), may hold values from -0.25 to 0.25
- w_value_up: float32 [512, 1024], P(None, 'head'), may hold values from -0.25 to 0.25
- w_out: float32 [1024, 2304], P('head'), may hold values from -0.1875 to 0.1875
Outputs:
- output: float32 [1024, 2304], P(('ctx', 'head'))
The draws below stay inside these ranges and needn't reach their ends.
All inputs are finite; a program needn't handle non-finite values.
Results may differ from the reference program's by a relative error of at most 0.0003.
Values sent between devices are 32-bit elements; how exact they have to be, the bound alone decides.
A program may use at most 64 MiB of HBM per device.

```python
import jax
import jax.numpy as jnp
from jax import lax

D = 2304
HEADS = 8
RANK = 512
SHARED = 64
NOPE = 128
VDIM = 128
TOKENS = 1024


def draw_hidden(key, part):
    base_key = jax.random.fold_in(jax.random.fold_in(key, 17), 0)
    values = jnp.clip(jax.random.normal(base_key, (TOKENS, D), jnp.float32), -4.0, 4.0)
    return values.astype(jnp.float32)


def level_of(rng, extent, shards, low, largest):
    level = 1.0
    for position, parts in shards:
        steps = jax.random.uniform(jax.random.fold_in(jax.random.fold_in(rng, 6), position), (parts,), jnp.float32, low / len(shards), largest / len(shards))
        level = level * jnp.repeat(jnp.exp(steps), extent[position] // parts).reshape((-1,) + (1,) * (len(extent) - 1 - position))
    return level


def centred(stream_key, dims, width, reach, cuts=(), kind=jnp.bfloat16):
    array = jax.random.normal(stream_key, dims, jnp.float32) * width
    if len(cuts) > 0:
        array = level_of(stream_key, dims, cuts, -0.22, 0.18) * array
    return jnp.clip(array, min=-reach, max=reach).astype(kind)


def setup_inputs(seed: int = 0) -> dict:
    key_of = jax.random.split(jax.random.key(seed), 8)
    hidden = draw_hidden(jax.random.fold_in(key_of[7], 71), 0)
    w_query = centred(key_of[1], (D, HEADS * (NOPE + SHARED)), D ** -0.5, 0.125, ((1, 8),), jnp.float32)
    w_down = centred(key_of[2], (D, RANK + SHARED), D ** -0.5, 0.125, (), jnp.float32)
    latent_gain = jnp.clip(1.0 + 0.15 * jax.random.normal(key_of[3], (RANK,), jnp.float32), 0.25, 1.75)
    w_key_up = centred(key_of[4], (RANK, HEADS * NOPE), RANK ** -0.5, 0.25, ((1, 8),), jnp.float32)
    w_value_up = centred(key_of[5], (RANK, HEADS * VDIM), RANK ** -0.5, 0.25, ((1, 8),), jnp.float32)
    w_out = centred(key_of[6], (HEADS * VDIM, D), (HEADS * VDIM) ** -0.5, 0.1875, ((0, 8),), jnp.float32)
    return dict(hidden=hidden, w_query=w_query, w_down=w_down, latent_gain=latent_gain, w_key_up=w_key_up, w_value_up=w_value_up, w_out=w_out)


EXACT = lax.Precision.HIGHEST

def matmul(left, right):
    return jnp.dot(left, right, precision=EXACT, preferred_element_type=jnp.float32)

def reference(hidden, w_query, w_down, latent_gain, w_key_up, w_value_up, w_out):
    down_part = matmul(hidden, w_down)
    raw_latent = down_part[:, :RANK]
    key_shared = down_part[:, RANK:]
    meansq = lax.optimization_barrier(jnp.mean(raw_latent * raw_latent, axis=-1, keepdims=True))
    latent = raw_latent * lax.rsqrt(meansq + 1e-06) * latent_gain
    queries = matmul(hidden, w_query).reshape(TOKENS, HEADS, NOPE + SHARED).transpose(1, 0, 2)
    key_own = matmul(latent, w_key_up).reshape(TOKENS, HEADS, NOPE).transpose(1, 0, 2)
    values = matmul(latent, w_value_up).reshape(TOKENS, HEADS, VDIM).transpose(1, 0, 2)
    positions = jnp.arange(TOKENS, dtype=jnp.int32)
    causal = positions[:, None] >= positions[None, :]
    score_scale = (NOPE + SHARED) ** (-0.5)

    def per_head(operands):
        head_query, head_key, head_value = operands
        scores = (matmul(head_query[:, :NOPE], head_key.T) + matmul(head_query[:, NOPE:], key_shared.T)) * score_scale
        scores = jnp.where(causal, scores, -jnp.inf)
        weights = jax.nn.softmax(scores, axis=-1)
        return matmul(weights, head_value)
    attended = lax.map(per_head, (queries, key_own, values))
    attended = attended.transpose(1, 0, 2).reshape(TOKENS, HEADS * VDIM)
    return matmul(attended, w_out)
```

```python
import functools

import jax
import jax.numpy as jnp
from jax import lax
from jax.experimental import pallas as pl
from jax.experimental.pallas import tpu as pltpu
from jax.sharding import PartitionSpec as P

EPSILON = 1e-06
FLOOR = -1e30
CORES = 2
MESH = pl.DeviceIdType.MESH
NN = (((1,), (0,)), ((), ()))
NT = (((1,), (1,)), ((), ()))


def halves(value):
    high = value.astype(jnp.bfloat16)
    return high, (value - high.astype(jnp.float32)).astype(jnp.bfloat16)


def product(left, right, dims=NN):
    (lh, ll), (rh, rl) = left, right
    dot = functools.partial(lax.dot_general, dimension_numbers=dims, preferred_element_type=jnp.float32)
    return dot(lh, rh) + (dot(ll, rh) + dot(lh, rl))


def divisor(extent, wish):
    while extent % wish:
        wish //= 2
    return wish


def kernel(
    ctx_n, chips, steps, pieces,
    hidden, w_query, w_down, gain, w_key, w_value, w_out, out,
    hid, wd, wq, gn, wk, wv, wo, lat, qh, ql, top, total, acc, part, landed,
    load_sem, swap_send, swap_recv, hid_send, hid_recv, col_send, col_recv,
    row_send, row_recv, twin_send, twin_recv, sum_send, sum_recv,
):
    rows, width = hidden.shape
    rank = gn.shape[1]
    tail = wd.shape[1] - rank
    nope = wk.shape[2]
    per_core = chips * rows
    block = CORES * per_core
    lanes = lat.shape[1]
    ctx = lax.axis_index("ctx")
    head = lax.axis_index("head")
    chip, core = head // CORES, head % CORES
    twin = chip * CORES + (1 - core)

    def chip_at(offset):
        return lax.rem(chip + offset, chips)

    def local(src, dst, sem):
        return pltpu.make_async_copy(src, dst, load_sem.at[sem])

    def remote(src, dst, send, recv, c, h):
        return pltpu.make_async_remote_copy(
            src_ref=src, dst_ref=dst, send_sem=send, recv_sem=recv,
            device_id={"ctx": c, "head": h}, device_id_type=MESH,
        )

    def at_rows(start, size):
        return pl.ds(pl.multiple_of(start, 8), size)

    my_hid = hid.at[at_rows(chip * rows, rows)]
    depth = width // steps
    loads = [local(hidden, my_hid, 0), local(gain, gn, 1)]
    for s in range(steps):
        loads.append(local(w_down.at[pl.ds(s * depth, depth)], wd.at[pl.ds(s * depth, depth)], 2 + s))
    pairs = [(w_query, wq), (w_key, wk), (w_value, wv), (w_out, wo)]
    own = [local(src, dst.at[core], 2 + steps + i) for i, (src, dst) in enumerate(pairs)]
    for copy in loads:
        copy.start()

    barrier = pltpu.get_barrier_semaphore()
    for o in range(1, chips):
        pl.semaphore_signal(barrier, inc=1, device_id={"ctx": ctx, "head": chip_at(o) * CORES + core}, device_id_type=MESH)
    pl.semaphore_signal(barrier, inc=1, device_id={"ctx": ctx, "head": twin}, device_id_type=MESH)
    for o in range(1, ctx_n):
        pl.semaphore_signal(barrier, inc=1, device_id={"ctx": lax.rem(ctx + o, ctx_n), "head": head}, device_id_type=MESH)
    pl.semaphore_wait(barrier, chips - 1 + 1 + ctx_n - 1)

    def hid_copy(o, k):
        return remote(hidden, hid.at[at_rows(k * rows, rows)], hid_send.at[o], hid_recv.at[k], ctx, chip_at(o) * CORES + core)

    for o in range(1, chips):
        hid_copy(o, chip).start()
    swaps = [remote(src, dst.at[core], swap_send.at[i], swap_recv.at[i], ctx, twin) for i, (src, dst) in enumerate(pairs)]
    for copy in own:
        copy.start()
    for copy in swaps:
        copy.start()

    loads[0].wait()
    loads[1].wait()
    down = jnp.zeros((rows, rank + tail), jnp.float32)
    for s in range(steps):
        loads[2 + s].wait()
        span = pl.ds(s * depth, depth)
        down += product(halves(my_hid[:, span]), halves(wd[span, :]))
    raw = down[:, :rank]
    meansq = jnp.mean(raw * raw, axis=-1, keepdims=True)
    blank = jnp.zeros((rows, lanes - rank - tail), jnp.float32)

    def place(b, p, k):
        return ((b * CORES + p) * chips + k) * rows

    mine = at_rows(place(ctx, core, chip), rows)
    lat[mine, :rank] = raw * lax.rsqrt(meansq + EPSILON) * gn[...]
    lat[mine, rank:] = jnp.concatenate([down[:, rank:], blank], axis=1)

    def col_copy(b):
        spot = lat.at[at_rows(place(b, core, chip), rows)]
        return remote(spot, spot, col_send.at[b], col_recv.at[b], jnp.minimum(ctx + 1, ctx_n - 1), head)

    def row_copy(b, o, k):
        spot = lat.at[at_rows(place(b, core, k), rows)]
        return remote(spot, spot, row_send.at[b, o], row_recv.at[b, k], ctx, chip_at(o) * CORES + core)

    def twin_copy(b, p):
        spot = lat.at[at_rows(place(b, p, 0), per_core)]
        return remote(spot, spot, twin_send.at[b], twin_recv.at[b], ctx, twin)

    def spread(b):
        @pl.when(ctx + 1 < ctx_n)
        def _():
            col_copy(b).start()

        for o in range(1, chips):
            row_copy(b, o, chip).start()

    def gather_rows(b):
        for o in range(1, chips):
            row_copy(b, 0, chip_at(o)).wait_recv()
        twin_copy(b, core).start()

    spread(ctx)
    for d in range(1, ctx_n):
        @pl.when(d <= ctx)
        def _():
            col_copy(ctx - d).wait_recv()
            spread(ctx - d)

    gather_rows(ctx)

    for o in range(1, chips):
        hid_copy(0, chip_at(o)).wait_recv()
    for i in range(2):
        own[i].wait()
        swaps[i].wait()
    scale = wq.shape[2] ** (-0.5)
    pad = jnp.zeros((per_core, lanes - rank - tail), jnp.float32)
    query = [jnp.zeros((per_core, wq.shape[2]), jnp.float32) for _ in range(CORES)]
    for s in range(steps):
        span = pl.ds(s * depth, depth)
        piece = halves(hid[:, span])
        for p in range(CORES):
            query[p] += product(piece, halves(wq[p, span, :]))
    for p in range(CORES):
        wide = product(halves(query[p][:, :nope] * scale), halves(wk[p]), NT)
        span = pl.ds(p * per_core, per_core)
        qh[span, :rank], ql[span, :rank] = halves(wide)
        qh[span, rank:], ql[span, rank:] = halves(jnp.concatenate([query[p][:, nope:] * scale, pad], axis=1))

    def spots(index, parity):
        inner = lax.rem(index, per_core)
        return (lax.div(inner, rows) * CORES + parity) * rows + lax.rem(inner, rows)

    def attend(b, first):
        keys = halves(lat[at_rows(place(b, 0, 0), block), :])
        scores = product((qh[...], ql[...]), keys, NT)
        if first:
            line = lax.broadcasted_iota(jnp.int32, (block, 1), 0)
            column = lax.broadcasted_iota(jnp.int32, (1, block), 1)
            causal = spots(line, core) >= spots(column, lax.div(column, per_core))
            scores = jnp.where(causal, scores, FLOOR)
            peak = jnp.max(scores, axis=1, keepdims=True)
        else:
            peak = jnp.maximum(top[...], jnp.max(scores, axis=1, keepdims=True))
        weights = jnp.exp(scores - peak)
        if first:
            weights = jnp.where(causal, weights, 0.0)
        mixed = product(halves(weights), (keys[0][:, :rank], keys[1][:, :rank]))
        added = jnp.sum(weights, axis=1, keepdims=True)
        if first:
            total[...] = added
            acc[...] = mixed
        else:
            fade = jnp.exp(top[...] - peak)
            total[...] = total[...] * fade + added
            acc[...] = acc[...] * fade + mixed
        top[...] = peak

    twin_copy(ctx, 1 - core).wait_recv()
    attend(ctx, True)
    for d in range(1, ctx_n):
        @pl.when(d <= ctx)
        def _():
            gather_rows(ctx - d)
            twin_copy(ctx - d, 1 - core).wait_recv()
            attend(ctx - d, False)

    for i in range(2, 4):
        own[i].wait()
        swaps[i].wait()
    heads = []
    for p in range(CORES):
        span = pl.ds(p * per_core, per_core)
        heads.append(product(halves(acc[span, :] / total[span, :]), halves(wv[p])))
    attended = halves(jnp.concatenate(heads, axis=1))
    columns = width // pieces

    def sum_copy(t, o, k):
        span = pl.ds(t * columns, columns)
        return remote(
            part.at[at_rows(chip_at(o) * rows, rows), span], landed.at[at_rows(k * rows, rows), span],
            sum_send.at[t, o], sum_recv.at[t, k], ctx, chip_at(o) * CORES + core,
        )

    for t in range(pieces):
        span = pl.ds(t * columns, columns)
        weight = jnp.concatenate([wo[p, :, span] for p in range(CORES)], axis=0)
        part[:, span] = product(attended, halves(weight))
        for o in range(1, chips):
            sum_copy(t, o, chip).start()
    for t in range(pieces):
        span = pl.ds(t * columns, columns)
        result = part[at_rows(chip * rows, rows), span]
        for o in range(1, chips):
            sum_copy(t, 0, chip_at(o)).wait_recv()
            result += landed[at_rows(chip_at(o) * rows, rows), span]
        out[:, span] = result

    for o in range(1, chips):
        hid_copy(o, chip).wait_send()
        for t in range(pieces):
            sum_copy(t, o, chip).wait_send()
    for d in range(ctx_n):
        @pl.when(d <= ctx)
        def _():
            @pl.when(ctx + 1 < ctx_n)
            def _():
                col_copy(ctx - d).wait_send()

            for o in range(1, chips):
                row_copy(ctx - d, o, chip).wait_send()
            twin_copy(ctx - d, core).wait_send()


def on_device(ctx_n, chips, hidden, w_query, w_down, latent_gain, w_key_up, w_value_up, w_out):
    rows, width = hidden.shape
    rank, nope = w_key_up.shape
    vdim = w_value_up.shape[1]
    per_core = chips * rows
    block = CORES * per_core
    lanes = -(-w_down.shape[1] // 128) * 128
    steps = 3 if width % 384 == 0 else 1
    pieces = 3 if width % 384 == 0 else 1
    f32, bf16, dma = jnp.float32, jnp.bfloat16, pltpu.SemaphoreType.DMA
    return pl.pallas_call(
        functools.partial(kernel, ctx_n, chips, steps, pieces),
        out_shape=jax.ShapeDtypeStruct((rows, width), f32),
        in_specs=[pl.BlockSpec(memory_space=pl.ANY)] * 7,
        out_specs=pl.BlockSpec(memory_space=pltpu.VMEM),
        scratch_shapes=[
            pltpu.VMEM((per_core, width), f32),
            pltpu.VMEM(w_down.shape, f32),
            pltpu.VMEM((CORES,) + w_query.shape, f32),
            pltpu.VMEM((1, rank), f32),
            pltpu.VMEM((CORES, rank, nope), f32),
            pltpu.VMEM((CORES, rank, vdim), f32),
            pltpu.VMEM((CORES, vdim, width), f32),
            pltpu.VMEM((ctx_n * block, lanes), f32),
            pltpu.VMEM((block, lanes), bf16),
            pltpu.VMEM((block, lanes), bf16),
            pltpu.VMEM((block, 1), f32),
            pltpu.VMEM((block, 1), f32),
            pltpu.VMEM((block, rank), f32),
            pltpu.VMEM((per_core, width), f32),
            pltpu.VMEM((per_core, width), f32),
            dma((2 + steps + 4,)),
            dma((4,)), dma((4,)),
            dma((chips,)), dma((chips,)),
            dma((ctx_n,)), dma((ctx_n,)),
            dma((ctx_n, chips)), dma((ctx_n, chips)),
            dma((ctx_n,)), dma((ctx_n,)),
            dma((pieces, chips)), dma((pieces, chips)),
        ],
        compiler_params=pltpu.CompilerParams(
            collective_id=0, has_side_effects=True, vmem_limit_bytes=56 * 1024 * 1024
        ),
    )(hidden, w_query, w_down, latent_gain.reshape(1, rank), w_key_up, w_value_up, w_out)


def solution(mesh):
    placed = (
        P(("ctx", "head"), None),
        P(None, "head"),
        P(),
        P(),
        P(None, "head"),
        P(None, "head"),
        P("head", None),
    )
    body = functools.partial(on_device, mesh.shape["ctx"], mesh.shape["head"] // CORES)
    return jax.shard_map(
        body, mesh=mesh, in_specs=placed, out_specs=P(("ctx", "head"), None), check_vma=False
    )
```

```python
import functools

import jax
import jax.numpy as jnp
from jax import lax
from jax.experimental import pallas as pl
from jax.experimental.pallas import tpu as pltpu
from jax.sharding import PartitionSpec as P

EPSILON = 1e-06
FLOOR = -1e30
CORES = 2
MESH = pl.DeviceIdType.MESH
NN = (((1,), (0,)), ((), ()))
NT = (((1,), (1,)), ((), ()))


def halves(value):
    high = value.astype(jnp.bfloat16)
    return high, (value - high.astype(jnp.float32)).astype(jnp.bfloat16)


def product(left, right, dims=NN):
    (lh, ll), (rh, rl) = left, right
    dot = functools.partial(lax.dot_general, dimension_numbers=dims, preferred_element_type=jnp.float32)
    return dot(lh, rh) + (dot(ll, rh) + dot(lh, rl))


def kernel(
    ctx_n, chips, square, steps, pieces,
    hidden, w_query, w_down, gain, w_key, w_value, w_out, out,
    hid, wd, wq, gn, wk, wv, wo, lat, qh, ql, top, total, acc, part, landed,
    load_sem, swap_send, swap_recv, hid_send, hid_recv, col_send, col_recv,
    row_send, row_recv, twin_send, twin_recv, sum_send, sum_recv,
):
    rows, width = hidden.shape
    parts = 2 if square else 1
    rank = gn.shape[1]
    tail = wd.shape[0] - rank
    nope = wk.shape[2]
    per_core = chips * rows
    block = CORES * per_core
    lanes = lat.shape[1]
    ctx = lax.axis_index("ctx")
    head = lax.axis_index("head")
    chip, core = head // CORES, head % CORES
    twin = chip * CORES + (1 - core)

    def chip_at(offset):
        return lax.rem(chip + offset, chips)

    def to(o):
        if not square:
            return chip_at(o)
        return [chip, chip + 1 - 2 * lax.rem(chip, 2), lax.rem(chip + 2, 4), 3 - chip][o]

    def origin(o):
        return to(o) if square else chip_at(chips - o)

    def local(src, dst, sem):
        return pltpu.make_async_copy(src, dst, load_sem.at[sem])

    def remote(src, dst, send, recv, c, h):
        return pltpu.make_async_remote_copy(
            src_ref=src, dst_ref=dst, send_sem=send, recv_sem=recv,
            device_id={"ctx": c, "head": h}, device_id_type=MESH,
        )

    def at_rows(start, size):
        return pl.ds(pl.multiple_of(start, 8), size)

    my_hid = hid.at[at_rows(chip * rows, rows)]
    depth = width // steps
    loads = [local(hidden, my_hid, 0), local(gain, gn, 1)]
    for s in range(steps):
        span = pl.ds(s * depth, depth)
        loads.append(local(w_down.at[:, span], wd.at[:, span], 2 + s))
    pairs = [(w_query, wq), (w_key, wk), (w_value, wv), (w_out, wo)]
    own = [local(src, dst.at[core], 2 + steps + i) for i, (src, dst) in enumerate(pairs)]
    for copy in loads:
        copy.start()

    barrier = pltpu.get_barrier_semaphore()
    for o in range(1, chips):
        pl.semaphore_signal(barrier, inc=1, device_id={"ctx": ctx, "head": chip_at(o) * CORES + core}, device_id_type=MESH)
    pl.semaphore_signal(barrier, inc=1, device_id={"ctx": ctx, "head": twin}, device_id_type=MESH)
    for o in range(1, ctx_n):
        pl.semaphore_signal(barrier, inc=1, device_id={"ctx": lax.rem(ctx + o, ctx_n), "head": head}, device_id_type=MESH)
    pl.semaphore_wait(barrier, chips - 1 + 1 + ctx_n - 1)

    def share(source, spot, send, recv):
        def start_of(o, h):
            target = to(o)
            return remote(source(h), spot(chip, h), send(o, h), recv(o, h), ctx, target * CORES + core)

        def seen(o, h):
            place_of = spot(origin(o), h)
            return remote(place_of, place_of, send(o, h), recv(o, h), ctx, twin)

        def passed(h):
            place_of = spot(to(1 + h), h)
            return remote(place_of, place_of, send(3, h), recv(3, h), ctx, to(2 - h) * CORES + core)

        direct = [(1, 0), (2, 1), (1, 1), (2, 0)] if square else [(o, 0) for o in range(1, chips)]

        def start():
            for o, h in direct:
                start_of(o, h).start()

        def relay():
            if square:
                for h in range(2):
                    seen(1 + h, h).wait_recv()
                    passed(h).start()

        def finish():
            for o, h in [(1, 1), (2, 0), (3, 0), (3, 1)] if square else direct:
                seen(o, h).wait_recv()

        def drain():
            for o, h in direct:
                start_of(o, h).wait_send()
            if square:
                for h in range(2):
                    passed(h).wait_send()

        return start, relay, finish, drain

    half = width // parts

    def hid_half(h):
        return pl.ds(h * half, half)

    hid_start, hid_relay, hid_finish, hid_drain = share(
        lambda h: hidden.at[:, hid_half(h)],
        lambda k, h: hid.at[at_rows(k * rows, rows), hid_half(h)],
        lambda o, h: hid_send.at[o, h],
        lambda o, h: hid_recv.at[o, h],
    )
    hid_start()
    swaps = [remote(src, dst.at[core], swap_send.at[i], swap_recv.at[i], ctx, twin) for i, (src, dst) in enumerate(pairs)]
    for copy in own:
        copy.start()
    for copy in swaps:
        copy.start()

    loads[0].wait()
    loads[1].wait()
    down = jnp.zeros((rows, rank + tail), jnp.float32)
    for s in range(steps):
        loads[2 + s].wait()
        span = pl.ds(s * depth, depth)
        down += product(halves(my_hid[:, span]), halves(wd[:, span]), NT)
    raw = down[:, :rank]
    meansq = jnp.mean(raw * raw, axis=-1, keepdims=True)
    blank = jnp.zeros((rows, lanes - rank - tail), jnp.float32)

    def place(b, p, k):
        return ((b * CORES + p) * chips + k) * rows

    mine = at_rows(place(ctx, core, chip), rows)
    lat[mine, :rank] = raw * lax.rsqrt(meansq + EPSILON) * gn[...]
    lat[mine, rank:] = jnp.concatenate([down[:, rank:], blank], axis=1)

    def col_copy(b):
        spot = lat.at[at_rows(place(b, core, chip), rows)]
        return remote(spot, spot, col_send.at[b], col_recv.at[b], jnp.minimum(ctx + 1, ctx_n - 1), head)

    def latents(b):
        def spot(k, h):
            return lat.at[at_rows(place(b, core, k) + h * (rows // parts), rows // parts)]

        return share(
            lambda h: spot(chip, h), spot, lambda o, h: row_send.at[b, o, h], lambda o, h: row_recv.at[b, o, h]
        )

    def twin_copy(b, p):
        spot = lat.at[at_rows(place(b, p, 0), per_core)]
        return remote(spot, spot, twin_send.at[b], twin_recv.at[b], ctx, twin)

    def spread(b):
        @pl.when(ctx + 1 < ctx_n)
        def _():
            col_copy(b).start()

        latents(b)[0]()

    def gather_rows(b):
        latents(b)[2]()
        twin_copy(b, core).start()

    spread(ctx)
    hid_relay()
    for d in range(1, ctx_n):
        @pl.when(d <= ctx)
        def _():
            col_copy(ctx - d).wait_recv()
            spread(ctx - d)

    latents(ctx)[1]()

    hid_finish()
    for i in range(2):
        own[i].wait()
        swaps[i].wait()
    scale = wq.shape[1] ** (-0.5)
    pad = jnp.zeros((per_core, lanes - rank - tail), jnp.float32)
    query = [jnp.zeros((per_core, wq.shape[1]), jnp.float32) for _ in range(CORES)]
    for s in range(steps):
        span = pl.ds(s * depth, depth)
        piece = halves(hid[:, span])
        for p in range(CORES):
            query[p] += product(piece, halves(wq[p, :, span]), NT)
    for p in range(CORES):
        wide = product(halves(query[p][:, :nope] * scale), halves(wk[p]), NT)
        span = pl.ds(p * per_core, per_core)
        qh[span, :rank], ql[span, :rank] = halves(wide)
        qh[span, rank:], ql[span, rank:] = halves(jnp.concatenate([query[p][:, nope:] * scale, pad], axis=1))

    def spots(index, parity):
        inner = lax.rem(index, per_core)
        return (lax.div(inner, rows) * CORES + parity) * rows + lax.rem(inner, rows)

    def attend(b, first):
        keys = halves(lat[at_rows(place(b, 0, 0), block), :])
        scores = product((qh[...], ql[...]), keys, NT)
        if first:
            line = lax.broadcasted_iota(jnp.int32, (block, 1), 0)
            column = lax.broadcasted_iota(jnp.int32, (1, block), 1)
            causal = spots(line, core) >= spots(column, lax.div(column, per_core))
            scores = jnp.where(causal, scores, FLOOR)
            peak = jnp.max(scores, axis=1, keepdims=True)
        else:
            peak = jnp.maximum(top[...], jnp.max(scores, axis=1, keepdims=True))
        weights = jnp.exp(scores - peak)
        if first:
            weights = jnp.where(causal, weights, 0.0)
        mixed = product(halves(weights), (keys[0][:, :rank], keys[1][:, :rank]))
        added = jnp.sum(weights, axis=1, keepdims=True)
        if first:
            total[...] = added
            acc[...] = mixed
        else:
            fade = jnp.exp(top[...] - peak)
            total[...] = total[...] * fade + added
            acc[...] = acc[...] * fade + mixed
        top[...] = peak

    def relay_at(d):
        if d < ctx_n:
            @pl.when(d <= ctx)
            def _():
                latents(ctx - d)[1]()

    relay_at(1)
    gather_rows(ctx)
    twin_copy(ctx, 1 - core).wait_recv()
    attend(ctx, True)
    for d in range(1, ctx_n):
        @pl.when(d <= ctx)
        def _():
            relay_at(d + 1)
            gather_rows(ctx - d)
            twin_copy(ctx - d, 1 - core).wait_recv()
            attend(ctx - d, False)

    for i in range(2, 4):
        own[i].wait()
        swaps[i].wait()
    heads = []
    for p in range(CORES):
        span = pl.ds(p * per_core, per_core)
        heads.append(product(halves(acc[span, :] / total[span, :]), halves(wv[p])))
    attended = halves(jnp.concatenate(heads, axis=1))
    columns = width // pieces

    def cut(ref, k, t):
        return ref.at[at_rows(k * rows, rows), pl.ds(t * columns, columns)]

    def axes_of(t):
        return (1, 2) if t % 2 == 0 else (2, 1)

    def sum_copy(t, j):
        if not square:
            return remote(
                cut(part, chip_at(j), t), cut(landed, chip, t), sum_send.at[t, j], sum_recv.at[t, j],
                ctx, chip_at(j) * CORES + core,
            )
        first, second = axes_of(t)
        src = [to(3), to(first), to(second)][j]
        dst = [to(3), to(first), to(3)][j]
        target = [to(first), to(first), to(second)][j]
        return remote(cut(part, src, t), cut(landed, dst, t), sum_send.at[t, j], sum_recv.at[t, j], ctx, target * CORES + core)

    def second_stage(t):
        sum_copy(t, 0).wait_recv()
        keep = to(axes_of(t)[1])
        cut(part, keep, t)[...] = cut(part, keep, t)[...] + cut(landed, keep, t)[...]
        sum_copy(t, 2).start()

    kinds = (0, 1) if square else tuple(range(1, chips))
    for t in range(pieces):
        span = pl.ds(t * columns, columns)
        weight = jnp.concatenate([wo[p, :, span] for p in range(CORES)], axis=0)
        part[:, span] = product(attended, halves(weight))
        for j in kinds:
            sum_copy(t, j).start()
        if square and t >= 2:
            second_stage(t - 2)
    if square:
        for t in range(max(pieces - 2, 0), pieces):
            second_stage(t)
    for t in range(pieces):
        result = cut(part, chip, t)[...]
        if square:
            for j in (1, 2):
                sum_copy(t, j).wait_recv()
            result += cut(landed, chip, t)[...] + cut(landed, to(axes_of(t)[0]), t)[...]
        else:
            for j in kinds:
                sum_copy(t, j).wait_recv()
                result += cut(landed, origin(j), t)[...]
        out[:, pl.ds(t * columns, columns)] = result

    hid_drain()
    for t in range(pieces):
        for j in kinds + ((2,) if square else ()):
            sum_copy(t, j).wait_send()
    for d in range(ctx_n):
        @pl.when(d <= ctx)
        def _():
            @pl.when(ctx + 1 < ctx_n)
            def _():
                col_copy(ctx - d).wait_send()

            latents(ctx - d)[3]()
            twin_copy(ctx - d, core).wait_send()


def on_device(ctx_n, chips, hidden, w_query, w_down, latent_gain, w_key_up, w_value_up, w_out):
    rows, width = hidden.shape
    rank, nope = w_key_up.shape
    vdim = w_value_up.shape[1]
    per_core = chips * rows
    block = CORES * per_core
    lanes = -(-w_down.shape[1] // 128) * 128
    steps = 3 if width % 384 == 0 else 1
    square = chips == 4 and rows % 16 == 0 and width % 256 == 0
    pieces = 6 if width % 768 == 0 else 2
    f32, bf16, dma = jnp.float32, jnp.bfloat16, pltpu.SemaphoreType.DMA
    return pl.pallas_call(
        functools.partial(kernel, ctx_n, chips, square, steps, pieces),
        out_shape=jax.ShapeDtypeStruct((rows, width), f32),
        in_specs=[pl.BlockSpec(memory_space=pltpu.HBM)] * 7,
        out_specs=pl.BlockSpec(memory_space=pltpu.VMEM),
        scratch_shapes=[
            pltpu.VMEM((per_core, width), f32),
            pltpu.VMEM(w_down.shape[::-1], f32),
            pltpu.VMEM((CORES,) + w_query.shape[::-1], f32),
            pltpu.VMEM((1, rank), f32),
            pltpu.VMEM((CORES, rank, nope), f32),
            pltpu.VMEM((CORES, rank, vdim), f32),
            pltpu.VMEM((CORES, vdim, width), f32),
            pltpu.VMEM((ctx_n * block, lanes), f32),
            pltpu.VMEM((block, lanes), bf16),
            pltpu.VMEM((block, lanes), bf16),
            pltpu.VMEM((block, 1), f32),
            pltpu.VMEM((block, 1), f32),
            pltpu.VMEM((block, rank), f32),
            pltpu.VMEM((per_core, width), f32),
            pltpu.VMEM((per_core, width), f32),
            dma((2 + steps + 4,)),
            dma((4,)), dma((4,)),
            dma((chips, 2)), dma((chips, 2)),
            dma((ctx_n,)), dma((ctx_n,)),
            dma((ctx_n, chips, 2)), dma((ctx_n, chips, 2)),
            dma((ctx_n,)), dma((ctx_n,)),
            dma((pieces, chips)), dma((pieces, chips)),
        ],
        compiler_params=pltpu.CompilerParams(
            collective_id=0, has_side_effects=True, vmem_limit_bytes=60 * 1024 * 1024
        ),
    )(hidden, w_query.T, w_down.T, latent_gain.reshape(1, rank), w_key_up, w_value_up, w_out)


def solution(mesh):
    placed = (
        P(("ctx", "head"), None),
        P(None, "head"),
        P(),
        P(),
        P(None, "head"),
        P(None, "head"),
        P("head", None),
    )
    body = functools.partial(on_device, mesh.shape["ctx"], mesh.shape["head"] // CORES)
    return jax.shard_map(
        body, mesh=mesh, in_specs=placed, out_specs=P(("ctx", "head"), None), check_vma=False
    )
```
